32 devices in a mesh: group: 2 (over x), expert: 16 (over z, y, core).
Axes of the slice: x: 2, y: 2, z: 4, core: 2. Of those that a mesh axis runs over, the one named last changes fastest.
Arguments:
- tokens: bfloat16 [4096, 7168], P(('group', 'expert')), parts along dimension 0, may hold values from -6 to 6
- expert_ids: int32 [4096, 2], P(('group', 'expert')), parts along dimension 0, may hold values from 0 to 7, all different within a row; in each aligned block of 128 rows (0 to 127, 128 to 255, ...) at most 64 rows name the same one
- gate_weights: float32 [4096, 2], P(('group', 'expert')), parts along dimension 0, may hold values from 0.05 to 1
- slot_expert: int32 [16], replicated, may hold values from 0 to 7, as said below
- w_gate_up: bfloat16 [16, 7168, 1024], P('expert'), may hold values from -0.0625 to 0.0625
- w_down: bfloat16 [16, 512, 7168], P('expert'), may hold values from -0.1875 to 0.1875
Outputs:
- moe_output: bfloat16 [4096, 7168], P(('group', 'expert')), parts along dimension 0
The draws below stay inside these ranges and needn't reach their ends.
There are 2 independent parts, one for each index of `group`. The reference program is written for one: setup_inputs(seed, part) draws one part's arguments, and reference() takes and returns one part's arrays. A program takes and returns all parts, laid end to end along the dimension named above; an argument that names none is the same for every part. Nothing has to cross between parts.
Inputs may be any that keep to these rules, and one draw needn't show every extreme that they name: `expert_ids`: each token names 2 different experts. In the rows of one device (128 tokens) no expert is named more than 64 times, a bound that some block reaches. `slot_expert`: the first 8 slots hold every expert once, and slot s + 8 holds the same expert as slot s.
All inputs are finite; a program needn't handle non-finite values.
Results may differ from the reference program's by a relative error of at most 0.0065.
Values may be sent and summed in bfloat16 or wider, within the bound.
A program may use at most 128 MiB of HBM per device.

```python
import math
import jax
import jax.numpy as jnp
import numpy as np
from jax import lax

D = 7168
FF = 1024
TOP = 2
TOK_DEV = 128
FSH = 512
EXPERTS = 8
MOST = 64
TOKENS = 2048
N_EXPERT = 16


def draw_slot_expert(key, part):
    order = jax.random.permutation(key, EXPERTS).astype(jnp.int32)
    return jnp.concatenate([order, order])


def block_levels(own_key, dims, cuts, least, high):
    factor_of = 1.0
    for position, parts in cuts:
        heights = jax.random.uniform(jax.random.fold_in(jax.random.fold_in(own_key, 6), position), (parts,), jnp.float32, least / len(cuts), high / len(cuts))
        factor_of = factor_of * jnp.repeat(jnp.exp(heights), dims[position] // parts).reshape((-1,) + (1,) * (len(dims) - 1 - position))
    return factor_of


def deal_out(own_key, own, number, rows, amount, top, most, lean):
    ranking = jax.random.permutation(own_key, amount)
    heavy_load, usual = load_shares(amount, rows * top, most, lean, True), load_shares(amount, rows * top, most, lean, False)
    places = jnp.arange(amount)

    def named(sizes, rotation):
        used = int((sizes > 0).sum())
        fixed = max(1, used // 4)
        passed = fixed + (places - fixed + rotation * (used - fixed)) % max(1, amount - fixed)
        return jnp.zeros((amount,), jnp.int32).at[ranking[jnp.where(places < fixed, places, passed)]].set(jnp.asarray(sizes, jnp.int32))

    sizes = jnp.where(number % 4 == 0, named(heavy_load, number // 4), named(usual, number - number // 4 - 1))
    mixed = jax.random.permutation(jax.random.fold_in(own, 3), amount)
    donor, taker = mixed[0:amount // 2 * 2:2], mixed[1:amount // 2 * 2:2]
    room = jnp.minimum(sizes[donor] - 1, most - sizes[taker]) // 2
    room = jnp.where((donor == ranking[0]) | (taker == ranking[0]) | (sizes[taker] == 0), 0, jnp.maximum(room, 0))
    passed = jax.random.randint(jax.random.fold_in(own, 4), (amount // 2,), 0, 1 << 20) % (room + 1)
    sizes = sizes.at[donor].add(-passed).at[taker].add(passed)
    members = jnp.searchsorted(jnp.cumsum(sizes), jnp.arange(rows * top), side="right").astype(jnp.int32)
    grid = members.reshape(top, rows).T
    grid = grid[jax.random.permutation(jax.random.fold_in(own, 1), rows)]
    rotation = jax.random.randint(jax.random.fold_in(own, 2), (rows, 1), 0, top)
    return jnp.take_along_axis(grid, (jnp.arange(top)[None, :] + rotation) % top, axis=1)


def load_shares(count, total, reach, skew, full):
    loads = [(1 << 20) // math.isqrt(rank ** skew) + 1 for rank in range(1, count + 1)]
    largest = reach if full else min(reach, max(-(-total // count), total * loads[0] // sum(loads)))
    least = 1 if total - largest >= count - 1 else 0
    given, rest = [largest] + [least] * (count - 1), total - largest - least * (count - 1)
    while rest > 0:
        free = [i for i in range(1, count) if given[i] < largest] or [i for i in range(1, count) if given[i] < reach]
        mass, remaining = sum([loads[i] for i in free]), rest
        for i in free:
            more = min(reach - given[i], max(1, remaining * loads[i] // mass), rest)
            given[i] = given[i] + more
            rest = rest - more
    return np.array(given)


def scatter_about(stream_key, extent, scale, most, split=(), kind=jnp.bfloat16):
    drawn = jax.random.normal(stream_key, extent, jnp.float32) * scale
    if len(split) > 0:
        drawn = block_levels(stream_key, extent, split, -0.22, 0.18) * drawn
    return jnp.clip(drawn, min=-most, max=most).astype(kind)


def setup_inputs(seed: int = 0, part: int = 0) -> dict:
    key_list = jax.random.split(jax.random.key(seed), 7)
    own_keys = jax.random.split(jax.random.fold_in(key_list[6], part), 7)
    tokens = scatter_about(own_keys[0], (TOKENS, D), 1.0, 6.0, ((0, 16),))
    expert_ids_keys = jax.random.split(jax.random.fold_in(own_keys[1], 1), TOKENS // TOK_DEV)
    expert_ids_turns = jax.random.permutation(jax.random.fold_in(own_keys[1], 3), TOKENS // TOK_DEV)
    expert_ids = jax.vmap(lambda own, number: deal_out(jax.random.fold_in(own_keys[1], 2), own, number, TOK_DEV, EXPERTS, TOP, MOST, 2))(expert_ids_keys, expert_ids_turns).reshape((TOKENS, TOP))
    gate_weights = jnp.clip(jnp.exp(math.log(1.0) - 2.9957323 * jax.random.uniform(own_keys[2], (TOKENS, TOP), jnp.float32) ** block_levels(own_keys[2], (TOKENS, TOP), ((0, 16),), -0.2, 0.2)), 0.05, 1.0)
    slot_expert = draw_slot_expert(jax.random.fold_in(key_list[6], 71), part)
    w_gate_up = scatter_about(key_list[4], (N_EXPERT, D, FF), D ** -0.5, 0.0625, ((0, 16),))
    w_down = scatter_about(key_list[5], (N_EXPERT, FSH, D), FF ** -0.5, 0.1875, ((0, 16),))
    return dict(tokens=tokens, expert_ids=expert_ids, gate_weights=gate_weights, slot_expert=slot_expert, w_gate_up=w_gate_up, w_down=w_down)


def reference(tokens, expert_ids, gate_weights, slot_expert, w_gate_up, w_down):
    choice_total = TOKENS * TOP
    span = N_EXPERT * MOST
    flat_ids = expert_ids.reshape(-1).astype(jnp.int32)
    order = jnp.argsort(flat_ids, stable=True).astype(jnp.int32)
    member = (flat_ids[:, None] == jnp.arange(EXPERTS, dtype=jnp.int32)[None, :]).astype(jnp.int32)
    counts = jnp.sum(member, axis=0).astype(jnp.int32)
    starts = (jnp.cumsum(counts) - counts).astype(jnp.int32)
    padded_order = jnp.concatenate([order, jnp.zeros((span,), jnp.int32)])

    def slot_half(rows, slot):
        projected = jnp.dot(rows, w_gate_up[slot], preferred_element_type=jnp.float32)
        hidden = (jax.nn.silu(projected[:, :FSH]) * projected[:, FSH:]).astype(jnp.bfloat16)
        return jnp.dot(hidden, w_down[slot], preferred_element_type=jnp.float32).astype(jnp.bfloat16)

    def one_expert(slot):
        expert = slot_expert[slot]
        picked = lax.dynamic_slice_in_dim(padded_order, starts[expert], span)
        valid = jnp.arange(span, dtype=jnp.int32) < counts[expert]
        rows = tokens[picked // TOP]
        lower = slot_half(rows, slot)
        upper = slot_half(rows, slot + EXPERTS)
        summed = (lower.astype(jnp.float32) + upper.astype(jnp.float32)).astype(jnp.bfloat16)
        summed = jnp.where(valid[:, None], summed, jnp.zeros_like(summed))
        target = jnp.where(valid, picked, choice_total).astype(jnp.int32)
        return summed, target

    outputs, targets = lax.map(one_expert, jnp.arange(EXPERTS, dtype=jnp.int32))
    table = jnp.zeros((choice_total + 1, D), jnp.bfloat16)
    table = table.at[targets.reshape(-1)].set(outputs.reshape(-1, D))
    chosen = table[:choice_total].reshape(TOKENS, TOP, D)
    total = jnp.sum(gate_weights[:, :, None] * chosen.astype(jnp.float32), axis=1)
    return total.astype(jnp.bfloat16)
```

```python
import jax
import jax.numpy as jnp
from jax import lax
from jax.sharding import PartitionSpec as P

CHUNKS = 1


def per_device(tokens, expert_ids, gate_weights, slot_expert, w_gate_up, w_down):
    devices = lax.axis_size("expert")
    experts = devices // 2
    rows, width = tokens.shape
    half = w_down.shape[1]
    chosen = expert_ids[:, :, None] == slot_expert[None, None, :experts]
    weights = jnp.sum(jnp.where(chosen, gate_weights[:, :, None], 0.0), axis=1)
    all_weights = lax.all_gather(weights, "expert", axis=0, tiled=False)
    column = lax.rem(lax.axis_index("expert"), experts)
    mine = lax.dynamic_index_in_dim(all_weights, column, axis=2, keepdims=False)
    step = rows // CHUNKS
    out = []
    for c in range(CHUNKS):
        part = lax.all_gather(tokens[c * step:(c + 1) * step], "expert", axis=0, tiled=True)
        w = mine[:, c * step:(c + 1) * step].reshape(-1, 1)
        projected = jnp.dot(part, w_gate_up[0], preferred_element_type=jnp.float32)
        hidden = jax.nn.silu(projected[:, :half]) * projected[:, half:] * w
        partial = jnp.dot(hidden.astype(jnp.bfloat16), w_down[0], preferred_element_type=jnp.float32).astype(jnp.bfloat16)
        out.append(lax.psum_scatter(partial, "expert", scatter_dimension=0, tiled=True))
    return jnp.concatenate(out, axis=0)


def solution(mesh):
    return jax.shard_map(
        per_device,
        mesh=mesh,
        in_specs=(
            P(("group", "expert"), None),
            P(("group", "expert"), None),
            P(("group", "expert"), None),
            P(),
            P("expert", None, None),
            P("expert", None, None),
        ),
        out_specs=P(("group", "expert"), None),
        check_vma=False,
    )
```

```python
import jax
import jax.numpy as jnp
import numpy as np
from jax import lax
from jax.sharding import PartitionSpec as P


def nearest(length):
    order = []
    for z in range(length):
        both = min(z, length - 1 - z)
        rest = [(t // 2 + 1, t % 2 == 0) for t in range(2 * both)]
        order.append(rest + [(t - both + 1, 2 * z > length - 1) for t in range(2 * both, length - 1)])
    return order


def pick(z, arrays, keys):
    out = arrays[keys[0]]
    for key in sorted(set(keys)):
        if key != keys[0]:
            hit = (z == np.array([i for i, k in enumerate(keys) if k == key])).any()
            out = jnp.where(hit, arrays[key], out)
    return out


def add(*terms):
    total = terms[0].astype(jnp.float32)
    for term in terms[1:]:
        total = total + term.astype(jnp.float32)
    return total.astype(jnp.bfloat16)


def per_device(tokens, expert_ids, gate_weights, slot_expert, w_gate_up, w_down):
    devices = lax.axis_size("expert")
    experts = devices // 2
    length = devices // 4
    rows, width = tokens.shape
    half = w_down.shape[1]
    me = lax.axis_index("expert")
    z, y, c = me // 4, me // 2 % 2, me % 2

    def line(x, step, who):
        return lax.ppermute(x, "expert", [(4 * i + j, 4 * (i + step) + j) for i in who for j in range(4)])

    def across(x):
        return lax.ppermute(x, "expert", [(i, i ^ 2) for i in range(devices)])

    def other_core(x):
        return lax.ppermute(x, "expert", [(i, i ^ 1) for i in range(devices)])

    chosen = expert_ids[:, :, None] == slot_expert[None, None, :experts]
    weights = jnp.sum(jnp.where(chosen, gate_weights[:, :, None], 0.0), axis=1)
    all_weights = lax.all_gather(weights, "expert", axis=0, tiled=False)
    mine = lax.dynamic_index_in_dim(all_weights, lax.rem(me, experts), axis=2, keepdims=False)

    order = nearest(length)
    arrived = {}
    up, down = tokens, tokens
    for s in range(1, length):
        up = line(up, 1, range(s - 1, length - 1))
        down = line(down, -1, range(1, length - s + 1))
        arrived[(s, True)], arrived[(s, False)] = up, down
    sums, homes = {}, []
    for t in range(-1, length - 1):
        if t < 0:
            block, home = tokens, z
        else:
            block = pick(z, arrived, [order[i][t] for i in range(length)])
            home = jnp.asarray([i - order[i][t][0] * (1 if order[i][t][1] else -1) for i in range(length)], jnp.int32)[z]
        over = across(block)
        group = jnp.concatenate([block, over, other_core(block), other_core(over)], axis=0)
        owners = [4 * home + 2 * a + b for a, b in ((y, c), (1 - y, c), (y, 1 - c), (1 - y, 1 - c))]
        w = jnp.concatenate([mine[i] for i in owners])[:, None]
        projected = jnp.dot(group, w_gate_up[0], preferred_element_type=jnp.float32)
        hidden = (jax.nn.silu(projected[:, :half]) * projected[:, half:]).astype(jnp.bfloat16)
        partial = (jnp.dot(hidden, w_down[0], preferred_element_type=jnp.float32) * w).astype(jnp.bfloat16)
        chip = add(partial[:2 * rows], other_core(partial[2 * rows:]))
        sums[t] = (chip[:rows], chip[rows:])
    for t in reversed(range(-1, length - 1)):
        sums[t] = add(sums[t][0], across(sums[t][1]))
    index = [{(s, d): t for t, (s, d) in enumerate(order[i])} for i in range(length)]
    from_below = from_above = None
    for s in reversed(range(1, length)):
        rise = pick(z, sums, [index[i].get((s, False), -1) for i in range(length)])
        fall = pick(z, sums, [index[i].get((s, True), -1) for i in range(length)])
        if from_below is not None:
            rise, fall = add(rise, from_below), add(fall, from_above)
        from_below = line(rise, 1, range(0, length - s))
        from_above = line(fall, -1, range(s, length))
    return add(sums[-1], from_below, from_above)


def solution(mesh):
    return jax.shard_map(
        per_device,
        mesh=mesh,
        in_specs=(
            P(("group", "expert"), None),
            P(("group", "expert"), None),
            P(("group", "expert"), None),
            P(),
            P("expert", None, None),
            P("expert", None, None),
        ),
        out_specs=P(("group", "expert"), None),
        check_vma=False,
    )
```

```python
import jax
import jax.numpy as jnp
import numpy as np
from jax import lax
from jax.sharding import PartitionSpec as P


def nearest(length):
    order = []
    for z in range(length):
        both = min(z, length - 1 - z)
        rest = [(t // 2 + 1, t % 2 == 0) for t in range(2 * both)]
        order.append(rest + [(t - both + 1, 2 * z > length - 1) for t in range(2 * both, length - 1)])
    return order


def pick(z, arrays, keys):
    out = arrays[keys[0]]
    for key in sorted(set(keys)):
        if key != keys[0]:
            hit = (z == np.array([i for i, k in enumerate(keys) if k == key])).any()
            out = jnp.where(hit, arrays[key], out)
    return out


def add(*terms):
    total = terms[0].astype(jnp.float32)
    for term in terms[1:]:
        total = total + term.astype(jnp.float32)
    return total.astype(jnp.bfloat16)


def per_device(tokens, expert_ids, gate_weights, slot_expert, w_gate_up, w_down):
    devices = lax.axis_size("expert")
    experts = devices // 2
    length = devices // 4
    rows, width = tokens.shape
    half = w_down.shape[1]
    me = lax.axis_index("expert")
    z, y, c = me // 4, me // 2 % 2, me % 2

    def line(x, step, who):
        return lax.ppermute(x, "expert", [(4 * i + j, 4 * (i + step) + j) for i in who for j in range(4)])

    def across(x):
        return lax.ppermute(x, "expert", [(i, i ^ 2) for i in range(devices)])

    def other_core(x):
        return lax.ppermute(x, "expert", [(i, i ^ 1) for i in range(devices)])

    chosen = expert_ids[:, :, None] == slot_expert[None, None, :experts]
    weights = jnp.sum(jnp.where(chosen, gate_weights[:, :, None], 0.0), axis=1)
    all_weights = lax.all_gather(weights, "expert", axis=0, tiled=False)
    mine = lax.dynamic_index_in_dim(all_weights, lax.rem(me, experts), axis=2, keepdims=False)

    order = nearest(length)
    mine, up, down = lax.optimization_barrier((mine, tokens, tokens))
    arrived, sums, chips = {}, {}, {}
    last = length - 2

    def halves(block, home):
        def rows_of(x, a):
            gates = jnp.concatenate([mine[4 * home + 2 * a + b] for b in (c, 1 - c)])
            return jnp.concatenate([x, other_core(x)], axis=0), gates[:, None]
        return rows_of(block, y), rows_of(across(block), 1 - y)

    def expert(parts):
        group = jnp.concatenate([part[0] for part in parts], axis=0)
        w = jnp.concatenate([part[1] for part in parts], axis=0)
        projected = jnp.dot(group, w_gate_up[0], preferred_element_type=jnp.float32)
        hidden = (jax.nn.silu(projected[:, :half]) * projected[:, half:]).astype(jnp.bfloat16)
        partial = (jnp.dot(hidden, w_down[0], preferred_element_type=jnp.float32) * w).astype(jnp.bfloat16)
        out = []
        for i in range(len(parts)):
            own = partial[2 * i * rows:(2 * i + 1) * rows]
            out.append(add(own, other_core(partial[(2 * i + 1) * rows:(2 * i + 2) * rows])))
        return out

    waiting, names = list(halves(tokens, z)), [(-1, 0), (-1, 1)]
    for s in range(1, length):
        up = line(up, 1, range(s - 1, length - 1))
        down = line(down, -1, range(1, length - s + 1))
        arrived[(s, True)], arrived[(s, False)] = up, down
        t = s - 1
        block = pick(z, arrived, [order[i][t] for i in range(length)])
        if t < last:
            block, up, down = lax.optimization_barrier((block, up, down))
        home = jnp.asarray([i - order[i][t][0] * (1 if order[i][t][1] else -1) for i in range(length)], jnp.int32)[z]
        near, far = halves(block, home)
        waiting.append(near)
        names.append((t, 0))
        if t < last:
            waiting.append(far)
            names.append((t, 1))
        if t != last - 1:
            chips.update(zip(names, expert(waiting)))
            waiting, names = [], []
    chips.update(zip([(last, 1)], expert([far])))
    got = None
    for t in [last - 1, last] + list(range(last - 2, -2, -1)):
        leave = chips[(t, 1)]
        if got is not None:
            leave, got = lax.optimization_barrier((leave, got))
            sums[before] = add(chips[(before, 0)], got)
        got, before = across(leave), t
    sums[before] = add(chips[(before, 0)], got)
    index = [{(s, d): t for t, (s, d) in enumerate(order[i])} for i in range(length)]
    from_below = from_above = None
    for s in reversed(range(1, length)):
        rise = pick(z, sums, [index[i].get((s, False), -1) for i in range(length)])
        fall = pick(z, sums, [index[i].get((s, True), -1) for i in range(length)])
        if from_below is not None:
            rise, fall = add(rise, from_below), add(fall, from_above)
        from_below = line(rise, 1, range(0, length - s))
        from_above = line(fall, -1, range(s, length))
    return add(sums[-1], from_below, from_above)


def solution(mesh):
    return jax.shard_map(
        per_device,
        mesh=mesh,
        in_specs=(
            P(("group", "expert"), None),
            P(("group", "expert"), None),
            P(("group", "expert"), None),
            P(),
            P("expert", None, None),
            P("expert", None, None),
        ),
        out_specs=P(("group", "expert"), None),
        check_vma=False,
    )
```

```python
import jax
import jax.numpy as jnp
import numpy as np
from jax import lax
from jax.sharding import PartitionSpec as P


def nearest(length):
    order = []
    for z in range(length):
        both = min(z, length - 1 - z)
        rest = [(t // 2 + 1, t % 2 == 0) for t in range(2 * both)]
        order.append(rest + [(t - both + 1, 2 * z > length - 1) for t in range(2 * both, length - 1)])
    return order


def pick(z, arrays, keys):
    out = arrays[keys[0]]
    for key in sorted(set(keys)):
        if key != keys[0]:
            hit = (z == np.array([i for i, k in enumerate(keys) if k == key])).any()
            out = jnp.where(hit, arrays[key], out)
    return out


def add(*terms):
    total = terms[0].astype(jnp.float32)
    for term in terms[1:]:
        total = total + term.astype(jnp.float32)
    return total.astype(jnp.bfloat16)


def per_device(tokens, expert_ids, gate_weights, slot_expert, w_gate_up, w_down):
    devices = lax.axis_size("expert")
    experts = devices // 2
    length = devices // 4
    rows, width = tokens.shape
    half = w_down.shape[1]
    me = lax.axis_index("expert")
    z, y, c = me // 4, me // 2 % 2, me % 2

    def line(x, step, who):
        return lax.ppermute(x, "expert", [(4 * i + j, 4 * (i + step) + j) for i in who for j in range(4)])

    def across(x):
        return lax.ppermute(x, "expert", [(i, i ^ 2) for i in range(devices)])

    def other_core(x):
        return lax.ppermute(x, "expert", [(i, i ^ 1) for i in range(devices)])

    chosen = expert_ids[:, :, None] == slot_expert[None, None, :experts]
    weights = jnp.sum(jnp.where(chosen, gate_weights[:, :, None], 0.0), axis=1)
    all_weights = lax.all_gather(weights, "expert", axis=0, tiled=False)
    mine = lax.dynamic_index_in_dim(all_weights, lax.rem(me, experts), axis=2, keepdims=False)

    order = nearest(length)
    mine, up, down = lax.optimization_barrier((mine, tokens, tokens))
    arrived, sums, chips = {}, {}, {}
    last = length - 2

    def halves(block, home):
        def rows_of(x, a):
            gates = jnp.concatenate([mine[4 * home + 2 * a + b] for b in (c, 1 - c)])
            return jnp.concatenate([x, other_core(x)], axis=0), gates[:, None]
        return rows_of(block, y), rows_of(across(block), 1 - y)

    def expert(parts):
        group = jnp.concatenate([part[0] for part in parts], axis=0)
        w = jnp.concatenate([part[1] for part in parts], axis=0)
        projected = jnp.dot(group, w_gate_up[0], preferred_element_type=jnp.float32)
        hidden = (jax.nn.silu(projected[:, :half]) * projected[:, half:]).astype(jnp.bfloat16)
        partial = (jnp.dot(hidden, w_down[0], preferred_element_type=jnp.float32) * w).astype(jnp.bfloat16)
        out = []
        for i in range(len(parts)):
            own = partial[2 * i * rows:(2 * i + 1) * rows]
            out.append(add(own, other_core(partial[(2 * i + 1) * rows:(2 * i + 2) * rows])))
        return out

    waiting, names = list(halves(tokens, z)), [(-1, 0), (-1, 1)]
    for s in range(1, length):
        up = line(up, 1, range(s - 1, length - 1))
        down = line(down, -1, range(1, length - s + 1))
        arrived[(s, True)], arrived[(s, False)] = up, down
        t = s - 1
        block = pick(z, arrived, [order[i][t] for i in range(length)])
        if t < last:
            block, up, down = lax.optimization_barrier((block, up, down))
        elif (-1, 0) in chips:
            block, chips[(-1, 0)] = lax.optimization_barrier((block, chips[(-1, 0)]))
        home = jnp.asarray([i - order[i][t][0] * (1 if order[i][t][1] else -1) for i in range(length)], jnp.int32)[z]
        near, far = halves(block, home)
        waiting.append(near)
        names.append((t, 0))
        if t < last:
            waiting.append(far)
            names.append((t, 1))
        if t != last - 1:
            chips.update(zip(names, expert(waiting)))
            waiting, names = [], []
    chips.update(zip([(last, 1)], expert([far])))
    index = [{(s, d): t for t, (s, d) in enumerate(order[i])} for i in range(length)]
    rising = {s: [index[i].get((s, False), last) for i in range(length)] for s in range(1, length)}
    falling = {s: [index[i].get((s, True), last) for i in range(length)] for s in range(1, length)}
    got, picked = None, {}

    def settle(t, got):
        sums[t] = add(chips[(t, 0)], got)
        ready = [s for s in rising if s not in picked and set(rising[s] + falling[s]) <= set(sums)]
        for s in reversed(ready):
            picked[s] = lax.optimization_barrier((pick(z, sums, rising[s]), pick(z, sums, falling[s])))
        return ready

    for t in [last - 1, last] + list(range(last - 2, -2, -1)):
        leave = chips[(t, 1)]
        if got is not None:
            leave, got = lax.optimization_barrier((leave, got))
            for s in settle(before, got):
                leave, picked[s] = lax.optimization_barrier((leave, picked[s]))
        got, before = across(leave), t
    settle(before, got)
    from_below = from_above = None
    for s in reversed(range(1, length)):
        rise, fall = picked[s]
        if from_below is not None:
            rise, fall = add(rise, from_below), add(fall, from_above)
        from_below = line(rise, 1, range(0, length - s))
        from_above = line(fall, -1, range(s, length))
    return add(sums[-1], from_below, from_above)


def solution(mesh):
    return jax.shard_map(
        per_device,
        mesh=mesh,
        in_specs=(
            P(("group", "expert"), None),
            P(("group", "expert"), None),
            P(("group", "expert"), None),
            P(),
            P("expert", None, None),
            P("expert", None, None),
        ),
        out_specs=P(("group", "expert"), None),
        check_vma=False,
    )
```
